128 devices in a mesh: site: 8 (over y, core), sector: 16 (over z, x).
Axes of the slice: x: 4, y: 4, z: 4, core: 2. Of those that a mesh axis runs over, the one named last changes fastest.
Arguments:
- held_env: float32 [8, 3, 16, 384, 384], P('site', None, 'sector'), may hold values from -6 to 6
- incoming: float32 [4, 3, 16, 384, 384], P(None, None, 'sector'), may hold values from -6 to 6
- states: float32 [8, 4, 16, 384, 384], P('site', None, 'sector'), may hold values from -0.3125 to 0.3125
- weight_table: float32 [16, 4, 3, 3], replicated, may hold values from -2 to 2
- site_kind: int32 [8], P('site'), may hold values from 0 to 15
- sector_sizes: int32 [16], replicated, may hold values from 1 to 384, 5376 in all
- charge_shift: int32 [4], replicated, may hold values from 0 to 2, as said below
Outputs:
- final_env: float32 [8, 3, 16, 384, 384], P('site', None, 'sector')
The draws below stay inside these ranges and needn't reach their ends.
Inputs may be any that keep to these rules, and one draw needn't show every extreme that they name: `charge_shift`: each of 0, 1 and 2 appears among the shifts. `sector_sizes`: the sizes sum to 5376; the largest equals 384.
All inputs are finite; a program needn't handle non-finite values.
Results may differ from the reference program's by a relative error of at most 0.00015.
Values sent between devices are 32-bit elements; how exact they have to be, the bound alone decides.
No kernel may reach another device: no remote copies, remote signals or barrier semaphores. Data moves between devices by JAX's collectives and lax.ppermute only.
A program may use at most 128 MiB of HBM per device.

```python
import math
import jax
import jax.numpy as jnp
import numpy as np
from jax import lax

BLOCK = 384
TERMS = 3
LOCAL = 4
KINDS = 16
TICKS = 4
SECTS = 16
CHAIN = 8
BOND = 5376


def draw_charge_shift(key, part):
    base = jnp.array([0, 1, 2], dtype=jnp.int32)
    extra = jax.random.randint(jax.random.fold_in(key, 11), (1,), 0, 3).astype(jnp.int32)
    values = jnp.concatenate([base, extra])
    return jax.random.permutation(jax.random.fold_in(key, 12), values)


def with_ends(drawn, rng, smallest, largest):
    place = [jax.random.randint(jax.random.fold_in(rng, axis), (), 0, length) for axis, length in enumerate(drawn.shape)]
    main_axis = drawn.shape.index(max(drawn.shape))
    next_to = place[:main_axis] + [(place[main_axis] + 1) % drawn.shape[main_axis]] + place[main_axis + 1:]
    return drawn.at[tuple(place)].set(smallest).at[tuple(next_to)].set(largest)


def levels(stream_key, dims, split, smallest, largest):
    level = 1.0
    for dim, shards_of in split:
        draws = jax.random.uniform(jax.random.fold_in(jax.random.fold_in(stream_key, 6), dim), (shards_of,), jnp.float32, smallest / len(split), largest / len(split))
        level = level * jnp.repeat(jnp.exp(draws), dims[dim] // shards_of).reshape((-1,) + (1,) * (len(dims) - 1 - dim))
    return level


def length_profile(count, total, limit, skew):
    portions = [(1 << 20) // math.isqrt(rank ** skew) + 1 for rank in range(2, count + 1)]
    rest, holding = total - limit - (count - 1), [1] * (count - 1)
    while rest > 0:
        candidates = [i for i in range(count - 1) if holding[i] < limit]
        whole, budget = sum([portions[i] for i in candidates]), rest
        for i in candidates:
            more = min(limit - holding[i], max(1, budget * portions[i] // whole), rest)
            holding[i] = holding[i] + more
            rest = rest - more
    return np.array([limit] + holding)


def ragged_sizes(key, count, total, bound, skew):
    if count == 2:
        one = jax.random.randint(key, (), max(1, total - bound), min(bound, total - 1) + 1)
        return jnp.stack([one, total - one])
    lengths = jnp.asarray(length_profile(count, total, bound, skew), jnp.int32)
    twos = (count - 1) // 2
    giver, sink = lengths[1:1 + 2 * twos:2], lengths[2:2 + 2 * twos:2]
    margin = jnp.minimum(giver - 1, bound - sink)
    passed = jax.random.randint(jax.random.fold_in(key, 1), (twos,), 0, 1 << 20) % (margin + 1)
    lengths = lengths.at[1:1 + 2 * twos:2].set(giver - passed).at[2:2 + 2 * twos:2].set(sink + passed)
    return lengths[jax.random.permutation(jax.random.fold_in(key, 2), count)]


def centred(rng, shape, spread, limit, split=(), kind=jnp.bfloat16):
    entries = jax.random.normal(rng, shape, jnp.float32) * spread
    if len(split) > 0:
        entries = levels(rng, shape, split, -0.22, 0.18) * entries
    return jnp.clip(entries, min=-limit, max=limit).astype(kind)


def setup_inputs(seed: int = 0) -> dict:
    key_list = jax.random.split(jax.random.key(seed), 8)
    held_env = centred(key_list[0], (CHAIN, TERMS, SECTS, BLOCK, BLOCK), 1.0, 6.0, ((0, 8), (2, 16)), jnp.float32)
    incoming = centred(key_list[1], (TICKS, TERMS, SECTS, BLOCK, BLOCK), 1.0, 6.0, ((2, 16),), jnp.float32)
    states = centred(key_list[2], (CHAIN, LOCAL, SECTS, BLOCK, BLOCK), BLOCK ** -0.5, 0.3125, ((0, 8), (2, 16)), jnp.float32)
    weight_table = centred(key_list[3], (KINDS, LOCAL, TERMS, TERMS), 0.4, 2.0, (), jnp.float32)
    site_kind = with_ends(jax.random.randint(key_list[4], (CHAIN,), 0, KINDS), jax.random.fold_in(key_list[4], 1), 0, KINDS - 1).astype(jnp.int32)
    sector_sizes = ragged_sizes(key_list[5], SECTS, BOND, BLOCK, 2).astype(jnp.int32)
    charge_shift = draw_charge_shift(jax.random.fold_in(key_list[7], 71), 0)
    return dict(held_env=held_env, incoming=incoming, states=states, weight_table=weight_table, site_kind=site_kind, sector_sizes=sector_sizes, charge_shift=charge_shift)


def masked_states(states_site, sector_sizes, charge_shift):
    rows = jnp.arange(BLOCK, dtype=jnp.int32)
    owners = jnp.arange(SECTS, dtype=jnp.int32)
    target = (owners[None, :] + charge_shift[:, None]) % SECTS
    live_in = sector_sizes[owners]
    live_out = sector_sizes[target]
    keep = (rows[None, None, :, None] < live_in[None, :, None, None]) & (rows[None, None, None, :] < live_out[:, :, None, None])
    return jnp.where(keep, states_site, jnp.float32(0.0))


def advance(env, states_site, kind, weight_table, sector_sizes, charge_shift):
    masked = masked_states(states_site, sector_sizes, charge_shift)
    weights = weight_table[kind]
    result = jnp.zeros_like(env)
    for state in range(LOCAL):
        tensor = masked[state]
        right = jnp.einsum('kqab,qbj->kqaj', env, tensor, precision=lax.Precision.HIGHEST)
        triple = jnp.einsum('qai,kqaj->kqij', tensor, right, precision=lax.Precision.HIGHEST)
        mixed = jnp.einsum('kl,kqij->lqij', weights[state], triple, precision=lax.Precision.HIGHEST)
        for offset in range(3):
            moved = jnp.roll(mixed, offset, axis=1)
            result = result + jnp.where(charge_shift[state] == offset, moved, jnp.float32(0.0))
    return result


def reference(held_env, incoming, states, weight_table, site_kind, sector_sizes, charge_shift):
    held = held_env
    for tick in range(TICKS):
        def one_site(index):
            return advance(held[index], states[index], site_kind[index], weight_table, sector_sizes, charge_shift)
        updated = lax.map(one_site, jnp.arange(CHAIN, dtype=jnp.int32))
        held = jnp.concatenate([incoming[tick][None], updated[:-1]], axis=0)
    return held
```

```python
import functools

import jax
import jax.numpy as jnp
from jax import lax
from jax.experimental import pallas as pl
from jax.experimental.pallas import tpu as pltpu
from jax.sharding import PartitionSpec as P

TICKS = 4
AXES = ("site", "sector")
LOW = 128
VMEM = pl.BlockSpec(memory_space=pltpu.VMEM)
SMEM = pl.BlockSpec(memory_space=pltpu.SMEM)
ANY = pl.BlockSpec(memory_space=pl.ANY)
PARAMS = pltpu.CompilerParams(vmem_limit_bytes=40 * 1024 * 1024)


def halves(value):
    high = value.astype(jnp.bfloat16)
    return high, (value - high.astype(jnp.float32)).astype(jnp.bfloat16)


def dot(left, right):
    return jnp.dot(left, right, preferred_element_type=jnp.float32)


def prepare_kernel(place, sizes, shifts, states_ref, plain_ref, turned_ref):
    state = pl.program_id(0)
    block = states_ref.shape[-1]
    owner = place[1]
    live_in = sizes[owner]
    live_out = sizes[lax.rem(owner + shifts[state], sizes.shape[0])]
    rows = lax.broadcasted_iota(jnp.int32, (block, block), 0)
    columns = lax.broadcasted_iota(jnp.int32, (block, block), 1)
    keep = (rows < live_in) & (columns < live_out)
    masked = jnp.where(keep, states_ref[...], jnp.float32(0.0))
    high, low = halves(masked)
    plain_ref[0:block, :] = high
    plain_ref[block : 2 * block, :] = low
    plain_ref[2 * block :, :] = high
    high, low = halves(masked.T)
    turned_ref[:, 0:block] = high
    turned_ref[:, block : 2 * block] = high
    turned_ref[:, 2 * block :] = low


def prepare(place, sizes, shifts, states):
    count, block = states.shape[1], states.shape[3]
    return pl.pallas_call(
        prepare_kernel,
        grid=(count,),
        in_specs=[
            SMEM,
            SMEM,
            SMEM,
            pl.BlockSpec((None, None, None, block, block), lambda s: (0, s, 0, 0, 0)),
        ],
        out_specs=[
            pl.BlockSpec((None, 3 * block, block), lambda s: (s, 0, 0)),
            pl.BlockSpec((None, block, 3 * block), lambda s: (s, 0, 0)),
        ],
        out_shape=[
            jax.ShapeDtypeStruct((count, 3 * block, block), jnp.bfloat16),
            jax.ShapeDtypeStruct((count, block, 3 * block), jnp.bfloat16),
        ],
        name="prepare",
    )(place, sizes, shifts, states)


def products(offset, place, shifts, weights, env_ref, plain_ref, turned_ref, store):
    terms = env_ref.shape[0]
    count = plain_ref.shape[0]

    def one_state(state, found):
        mine = shifts[state] == offset

        @pl.when(mine)
        def _():
            base = (place[2] * count + state) * terms * terms
            for out_term in range(terms):
                mixed = weights[base + out_term] * env_ref[0]
                for term in range(1, terms):
                    mixed += weights[base + term * terms + out_term] * env_ref[term]
                high, low = halves(mixed)
                right = dot(turned_ref[state], jnp.concatenate([high, low, high], axis=0))
                high, low = halves(right)
                triple = dot(jnp.concatenate([high, high, low], axis=1), plain_ref[state])
                store(out_term, triple, found == 0)

        return found + mine.astype(jnp.int32)

    lax.fori_loop(0, count, one_state, jnp.int32(0))


def split_store(low_ref, high_ref):
    def store(term, value, first):
        @pl.when(first)
        def _():
            low_ref[term] = value[:LOW]
            high_ref[term] = value[LOW:]

        @pl.when(jnp.logical_not(first))
        def _():
            low_ref[term] += value[:LOW]
            high_ref[term] += value[LOW:]

    return store


def whole_store(ref):
    def store(term, value, first):
        @pl.when(first)
        def _():
            ref[term] = value

        @pl.when(jnp.logical_not(first))
        def _():
            ref[term] += value

    return store


def gather_kernel(tick, place, shifts, weights, stay, low, high, far, incoming, plain, turned,
                  out_low, out_high, env):
    @pl.when(place[0] == 0)
    def _():
        pltpu.sync_copy(incoming.at[tick, :, 0], env)

    @pl.when(place[0] != 0)
    def _():
        env[:, :LOW] = stay[:, :LOW] + low[...]
        env[:, LOW:] = stay[:, LOW:] + high[...] + far[...]

    products(2, place, shifts, weights, env, plain, turned, split_store(out_low, out_high))


def first_kernel(place, shifts, weights, env, plain, turned, out_low, out_high):
    products(2, place, shifts, weights, env, plain, turned, split_store(out_low, out_high))


def one_kernel(place, shifts, weights, env, plain, turned, out_low, out_high):
    products(1, place, shifts, weights, env, plain, turned, split_store(out_low, out_high))


def zero_kernel(place, shifts, weights, env, plain, turned, out):
    products(0, place, shifts, weights, env, plain, turned, whole_store(out))


def final_kernel(tick, place, stay, low, high, far, incoming, env):
    @pl.when(place[0] == 0)
    def _():
        pltpu.sync_copy(incoming.at[tick, :, 0], env)

    @pl.when(place[0] != 0)
    def _():
        env[:, :LOW] = stay[:, :LOW] + low[...]
        env[:, LOW:] = stay[:, LOW:] + high[...] + far[...]


def shape(*dims):
    return jax.ShapeDtypeStruct(dims, jnp.float32)


def estimate(block, terms):
    return pl.CostEstimate(
        flops=terms * 12 * block**3, bytes_accessed=16 * block * block * terms, transcendentals=0
    )


def routes(tick, columns, sites, sectors):
    relay, lift, far_one, far_two, stay = [], [], [], [], []
    for site in range(min(sites - 1, tick + TICKS)):
        for sector in range(sectors):
            here = site * sectors + sector
            after = (sector + 1) % sectors
            relay.append((here, site * sectors + after))
            lift.append((here, (site + 1) * sectors + after))
            stay.append((here, (site + 1) * sectors + sector))
            target = (sector + 2) % sectors
            back = (target // columns) * columns + (target + 1) % columns
            far_one.append((here, site * sectors + back))
            far_two.append((site * sectors + back, (site + 1) * sectors + target))
    return relay, lift, far_one, far_two, stay


def local(sites, held_env, incoming, states, weight_table, site_kind, sector_sizes, charge_shift):
    terms, block = held_env.shape[1], held_env.shape[3]
    sectors = sector_sizes.shape[0]
    columns = 4
    place = jnp.stack(
        [lax.axis_index("site"), lax.axis_index("sector"), site_kind[0]]
    ).astype(jnp.int32)
    weights = weight_table.reshape(-1)
    plain, turned = prepare(place, sector_sizes, charge_shift, states)
    env = held_env[0, :, 0]
    parts = [shape(terms, LOW, block), shape(terms, block - LOW, block)]
    cost = estimate(block, terms)
    moved = None
    for tick in range(TICKS + 1):
        if tick == TICKS:
            env = pl.pallas_call(
                functools.partial(final_kernel, tick - 1),
                in_specs=[SMEM] + [VMEM] * 4 + [ANY],
                out_specs=VMEM,
                out_shape=shape(terms, block, block),
                compiler_params=PARAMS,
                name="final",
            )(place, *moved, incoming)
            break
        if tick == 0:
            two_low, two_high = pl.pallas_call(
                first_kernel,
                in_specs=[SMEM] * 3 + [VMEM] * 3,
                out_specs=[VMEM] * 2,
                out_shape=parts,
                compiler_params=PARAMS,
                cost_estimate=cost,
                name="first",
            )(place, charge_shift, weights, env, plain, turned)
        else:
            two_low, two_high, env = pl.pallas_call(
                functools.partial(gather_kernel, tick - 1),
                in_specs=[SMEM] * 3 + [VMEM] * 4 + [ANY] + [VMEM] * 2,
                out_specs=[VMEM] * 3,
                out_shape=parts + [shape(terms, block, block)],
                compiler_params=PARAMS,
                cost_estimate=cost,
                name="gather",
            )(place, charge_shift, weights, *moved, incoming, plain, turned)
        relay, lift, far_one, far_two, stay = routes(tick, columns, sites, sectors)
        two_low = lax.ppermute(two_low, AXES, relay)
        far = lax.ppermute(two_high, AXES, far_one)
        one_low, one_high = pl.pallas_call(
            one_kernel,
            in_specs=[SMEM] * 3 + [VMEM] * 3,
            out_specs=[VMEM] * 2,
            out_shape=parts,
            compiler_params=PARAMS,
            cost_estimate=cost,
            name="one",
        )(place, charge_shift, weights, env, plain, turned)
        high = lax.ppermute(one_high, AXES, lift)
        zero = pl.pallas_call(
            zero_kernel,
            in_specs=[SMEM] * 3 + [VMEM] * 3,
            out_specs=VMEM,
            out_shape=shape(terms, block, block),
            compiler_params=PARAMS,
            cost_estimate=cost,
            name="zero",
        )(place, charge_shift, weights, env, plain, turned)
        kept = lax.ppermute(zero, AXES, stay)
        low = lax.ppermute(one_low + two_low, AXES, lift)
        far = lax.ppermute(far, AXES, far_two)
        moved = (kept, low, high, far)
    return env[None, :, None]


def solution(mesh):
    return jax.shard_map(
        functools.partial(local, mesh.shape["site"]),
        mesh=mesh,
        in_specs=(
            P("site", None, "sector", None, None),
            P(None, None, "sector", None, None),
            P("site", None, "sector", None, None),
            P(),
            P("site"),
            P(),
            P(),
        ),
        out_specs=P("site", None, "sector", None, None),
        check_vma=False,
    )
```

```python
import functools

import jax
import jax.numpy as jnp
from jax import lax
from jax.experimental import pallas as pl
from jax.experimental.pallas import tpu as pltpu
from jax.sharding import PartitionSpec as P


TICKS = 4
AXES = ("site", "sector")
LOW = 144
VMEM = pl.BlockSpec(memory_space=pltpu.VMEM)
SMEM = pl.BlockSpec(memory_space=pltpu.SMEM)
HBM = pl.BlockSpec(memory_space=pltpu.HBM)
PARAMS = pltpu.CompilerParams(vmem_limit_bytes=24 * 1024 * 1024)


def halves(value):
    high = value.astype(jnp.bfloat16)
    return high, (value - high.astype(jnp.float32)).astype(jnp.bfloat16)


def dot(left, right):
    return jnp.dot(left, right, preferred_element_type=jnp.float32)


def shift_of(place, state):
    return place[3 + state]


def fill(state, place, count, states_ref, plain_ref, turned_ref):
    block = states_ref.shape[-1]
    owner = place[1]
    sectors = place.shape[0] - 3 - count
    live_in = place[3 + count + owner]
    live_out = place[3 + count + lax.rem(owner + shift_of(place, state), sectors)]
    rows = lax.broadcasted_iota(jnp.int32, (block, block), 0)
    columns = lax.broadcasted_iota(jnp.int32, (block, block), 1)
    keep = (rows < live_in) & (columns < live_out)
    masked = jnp.where(keep, states_ref[0, state, 0], jnp.float32(0.0))
    high, low = halves(masked)
    plain_ref[state, 0:block, :] = high
    plain_ref[state, block : 2 * block, :] = low
    plain_ref[state, 2 * block :, :] = high
    high, low = halves(masked.T)
    turned_ref[state, :, 0:block] = high
    turned_ref[state, :, block : 2 * block] = high
    turned_ref[state, :, 2 * block :] = low


def products(offset, place, weights, env_ref, plain_ref, turned_ref, store, ready=None):
    terms = env_ref.shape[0]
    count = plain_ref.shape[0]

    def one_state(state, found):
        mine = shift_of(place, state) == offset

        @pl.when(mine)
        def _():
            if ready is not None:
                ready(state)
            base = (place[2] * count + state) * terms * terms

            def one_term(out_term):
                mixed = weights[base + out_term] * env_ref[0]
                for term in range(1, terms):
                    mixed += weights[base + term * terms + out_term] * env_ref[term]
                high, low = halves(mixed)
                right = dot(turned_ref[state], jnp.concatenate([high, low, high], axis=0))
                high, low = halves(right)
                triple = dot(jnp.concatenate([high, high, low], axis=1), plain_ref[state])
                store(out_term, triple, found == 0)

            pl.loop(0, terms)(one_term)

        return found + mine.astype(jnp.int32)

    lax.fori_loop(0, count, one_state, jnp.int32(0))


def split_store(low_ref, high_ref):
    def store(term, value, first):
        @pl.when(first)
        def _():
            low_ref[term] = value[:LOW]
            high_ref[term] = value[LOW:]

        @pl.when(jnp.logical_not(first))
        def _():
            low_ref[term] += value[:LOW]
            high_ref[term] += value[LOW:]

    return store


def whole_store(ref):
    def store(term, value, first):
        @pl.when(first)
        def _():
            ref[term] = value

        @pl.when(jnp.logical_not(first))
        def _():
            ref[term] += value

    return store


def gather_kernel(tick, place, weights, stay, low, high, far, incoming, plain, turned,
                  out_low, out_high, env):
    @pl.when(place[0] == 0)
    def _():
        pltpu.sync_copy(incoming.at[tick, :, 0], env)

    @pl.when(place[0] != 0)
    def _():
        env[:, :LOW] = stay[:, :LOW] + low[...]
        env[:, LOW:] = stay[:, LOW:] + high[...] + far[...]

    products(2, place, weights, env, plain, turned, split_store(out_low, out_high))


def first_kernel(place, weights, env, states, out_low, out_high, plain, turned):
    def ready(state):
        fill(state, place, plain.shape[0], states, plain, turned)

    products(2, place, weights, env, plain, turned, split_store(out_low, out_high), ready)


def first_one_kernel(place, weights, env, states, plain_in, turned_in,
                     out_low, out_high, plain, turned):
    def ready(state):
        fill(state, place, plain.shape[0], states, plain, turned)

    products(1, place, weights, env, plain, turned, split_store(out_low, out_high), ready)


def first_zero_kernel(place, weights, env, states, plain_in, turned_in,
                      out, plain, turned):
    def ready(state):
        fill(state, place, plain.shape[0], states, plain, turned)

    products(0, place, weights, env, plain, turned, whole_store(out), ready)


def one_kernel(place, weights, env, plain, turned, out_low, out_high):
    products(1, place, weights, env, plain, turned, split_store(out_low, out_high))


def zero_kernel(place, weights, env, plain, turned, out):
    products(0, place, weights, env, plain, turned, whole_store(out))


def final_kernel(tick, place, stay, low, high, far, incoming, env):
    @pl.when(place[0] == 0)
    def _():
        pltpu.sync_copy(incoming.at[tick, :, 0], env)

    @pl.when(place[0] != 0)
    def _():
        env[:, :LOW] = stay[:, :LOW] + low[...]
        env[:, LOW:] = stay[:, LOW:] + high[...] + far[...]


def shape(*dims):
    return jax.ShapeDtypeStruct(dims, jnp.float32)


def estimate(block, terms):
    return pl.CostEstimate(
        flops=terms * 12 * block**3, bytes_accessed=16 * block * block * terms, transcendentals=0
    )


def routes(tick, columns, sites, sectors):
    relay, lift, far_one, far_two, stay = [], [], [], [], []
    for site in range(min(sites - 1, tick + TICKS)):
        for sector in range(sectors):
            here = site * sectors + sector
            after = (sector + 1) % sectors
            relay.append((here, site * sectors + after))
            lift.append((here, (site + 1) * sectors + after))
            stay.append((here, (site + 1) * sectors + sector))
            target = (sector + 2) % sectors
            back = (target // columns) * columns + (target + 1) % columns
            far_one.append((here, site * sectors + back))
            far_two.append((site * sectors + back, (site + 1) * sectors + target))
    return relay, lift, far_one, far_two, stay


def local(sites, held_env, incoming, states, weight_table, site_kind, sector_sizes, charge_shift):
    terms, block = held_env.shape[1], held_env.shape[3]
    sectors = sector_sizes.shape[0]
    columns = 4
    here = jnp.stack([lax.axis_index("site"), lax.axis_index("sector")]).astype(jnp.int32)
    place = jnp.concatenate([here, site_kind, charge_shift, sector_sizes])
    weights = weight_table.reshape(-1)
    count = states.shape[1]
    env = held_env[0, :, 0]
    parts = [shape(terms, LOW, block), shape(terms, block - LOW, block)]
    whole = shape(terms, block, block)
    split_states = [
        jax.ShapeDtypeStruct((count, 3 * block, block), jnp.bfloat16),
        jax.ShapeDtypeStruct((count, block, 3 * block), jnp.bfloat16),
    ]
    cost = estimate(block, terms)
    scalars = (place, weights)
    few = (place, weights)
    plain, turned, moved = None, None, None

    def call(kernel, inputs, outputs, aliases={}):
        specs = [SMEM if value.ndim == 1 else VMEM for value in inputs]
        specs = [HBM if value is incoming else spec for spec, value in zip(specs, inputs)]
        return pl.pallas_call(
            kernel,
            in_specs=specs,
            out_specs=[VMEM] * len(outputs),
            out_shape=outputs,
            input_output_aliases=aliases,
            compiler_params=PARAMS,
            cost_estimate=cost,
        )(*inputs)

    for tick in range(TICKS):
        relay, lift, far_one, far_two, stay = routes(tick, columns, sites, sectors)
        if tick == 0:
            two_low, two_high, plain, turned = call(
                first_kernel, scalars + (env, states), parts + split_states
            )
        else:
            two_low, two_high, env = call(
                functools.partial(gather_kernel, tick - 1),
                few + moved + (incoming, plain, turned),
                parts + [whole],
            )
        two_low = lax.ppermute(two_low, AXES, relay)
        far = lax.ppermute(two_high, AXES, far_one)
        if tick == 0:
            zero, plain, turned = call(
                first_zero_kernel,
                scalars + (env, states, plain, turned),
                [whole] + split_states,
                {4: 1, 5: 2},
            )
        else:
            (zero,) = call(zero_kernel, few + (env, plain, turned), [whole])
        kept = lax.ppermute(zero, AXES, stay)
        if tick == 0:
            one_low, one_high, plain, turned = call(
                first_one_kernel,
                scalars + (env, states, plain, turned),
                parts + split_states,
                {4: 2, 5: 3},
            )
        else:
            one_low, one_high = call(one_kernel, few + (env, plain, turned), parts)
        high = lax.ppermute(one_high, AXES, lift)
        low = lax.ppermute(one_low + two_low, AXES, lift)
        far = lax.ppermute(far, AXES, far_two)
        moved = (kept, low, high, far)
    (env,) = call(
        functools.partial(final_kernel, TICKS - 1), (place,) + moved + (incoming,), [whole]
    )
    return env[None, :, None]


def solution(mesh):
    return jax.shard_map(
        functools.partial(local, mesh.shape["site"]),
        mesh=mesh,
        in_specs=(
            P("site", None, "sector", None, None),
            P(None, None, "sector", None, None),
            P("site", None, "sector", None, None),
            P(),
            P("site"),
            P(),
            P(),
        ),
        out_specs=P("site", None, "sector", None, None),
        check_vma=False,
    )
```

```python
import functools

import jax
import jax.numpy as jnp
from jax import lax
from jax.experimental import pallas as pl
from jax.experimental.pallas import tpu as pltpu
from jax.sharding import PartitionSpec as P


TICKS = 4
AXES = ("site", "sector")
LOW = 136
VMEM = pl.BlockSpec(memory_space=pltpu.VMEM)
SMEM = pl.BlockSpec(memory_space=pltpu.SMEM)
HBM = pl.BlockSpec(memory_space=pltpu.HBM)
PARAMS = pltpu.CompilerParams(vmem_limit_bytes=24 * 1024 * 1024)


def halves(value):
    high = value.astype(jnp.bfloat16)
    return high, (value - high.astype(jnp.float32)).astype(jnp.bfloat16)


def dot(left, right):
    return jnp.dot(left, right, preferred_element_type=jnp.float32)


def shift_of(place, state):
    return place[3 + state]


def fill(state, place, count, states_ref, plain_ref, turned_ref):
    block = states_ref.shape[-1]
    owner = place[1]
    sectors = place.shape[0] - 3 - count
    live_in = place[3 + count + owner]
    live_out = place[3 + count + lax.rem(owner + shift_of(place, state), sectors)]
    rows = lax.broadcasted_iota(jnp.int32, (block, block), 0)
    columns = lax.broadcasted_iota(jnp.int32, (block, block), 1)
    keep = (rows < live_in) & (columns < live_out)
    masked = jnp.where(keep, states_ref[0, state, 0], jnp.float32(0.0))
    high, low = halves(masked)
    plain_ref[state, 0:block, :] = high
    plain_ref[state, block : 2 * block, :] = low
    plain_ref[state, 2 * block :, :] = high
    high, low = halves(masked.T)
    turned_ref[state, :, 0:block] = high
    turned_ref[state, :, block : 2 * block] = high
    turned_ref[state, :, 2 * block :] = low


def products(offset, place, weights, env_ref, plain_ref, turned_ref, store, ready=None):
    terms = env_ref.shape[0]
    count = plain_ref.shape[0]

    def one_state(state, found):
        mine = shift_of(place, state) == offset

        @pl.when(mine)
        def _():
            if ready is not None:
                ready(state)
            base = (place[2] * count + state) * terms * terms

            def one_term(out_term):
                mixed = weights[base + out_term] * env_ref[0]
                for term in range(1, terms):
                    mixed += weights[base + term * terms + out_term] * env_ref[term]
                high, low = halves(mixed)
                right = dot(turned_ref[state], jnp.concatenate([high, low, high], axis=0))
                high, low = halves(right)
                triple = dot(jnp.concatenate([high, high, low], axis=1), plain_ref[state])
                store(out_term, triple, found == 0)

            pl.loop(0, terms)(one_term)

        return found + mine.astype(jnp.int32)

    lax.fori_loop(0, count, one_state, jnp.int32(0))


def split_store(low_ref, high_ref):
    def store(term, value, first):
        low, high = low_ref[term], high_ref[term]
        low_ref[term] = jnp.where(first, jnp.float32(0.0), low) + value[:LOW]
        high_ref[term] = jnp.where(first, jnp.float32(0.0), high) + value[LOW:]

    return store


def whole_store(ref):
    def store(term, value, first):
        ref[term] = jnp.where(first, jnp.float32(0.0), ref[term]) + value

    return store


def gather_kernel(tick, place, weights, stay, low, high, far, incoming, plain, turned,
                  out_low, out_high, env):
    @pl.when(place[0] == 0)
    def _():
        pltpu.sync_copy(incoming.at[tick, :, 0], env)

    @pl.when(place[0] != 0)
    def _():
        env[:, :LOW] = stay[:, :LOW] + low[...]
        env[:, LOW:] = stay[:, LOW:] + high[...] + far[...]

    products(2, place, weights, env, plain, turned, split_store(out_low, out_high))


def first_kernel(place, weights, env, states, out_low, out_high, plain, turned):
    def ready(state):
        fill(state, place, plain.shape[0], states, plain, turned)

    products(2, place, weights, env, plain, turned, split_store(out_low, out_high), ready)


def first_one_kernel(place, weights, env, states, plain_in, turned_in,
                     out_low, out_high, plain, turned):
    def ready(state):
        fill(state, place, plain.shape[0], states, plain, turned)

    products(1, place, weights, env, plain, turned, split_store(out_low, out_high), ready)


def first_zero_kernel(place, weights, env, states, plain_in, turned_in,
                      out, plain, turned):
    def ready(state):
        fill(state, place, plain.shape[0], states, plain, turned)

    products(0, place, weights, env, plain, turned, whole_store(out), ready)


def one_kernel(place, weights, env, plain, turned, out_low, out_high):
    products(1, place, weights, env, plain, turned, split_store(out_low, out_high))


def zero_kernel(place, weights, env, plain, turned, out):
    products(0, place, weights, env, plain, turned, whole_store(out))


def final_kernel(tick, place, stay, low, high, far, incoming, env):
    @pl.when(place[0] == 0)
    def _():
        pltpu.sync_copy(incoming.at[tick, :, 0], env)

    @pl.when(place[0] != 0)
    def _():
        env[:, :LOW] = stay[:, :LOW] + low[...]
        env[:, LOW:] = stay[:, LOW:] + high[...] + far[...]


def shape(*dims):
    return jax.ShapeDtypeStruct(dims, jnp.float32)


def estimate(block, terms):
    return pl.CostEstimate(
        flops=terms * 12 * block**3, bytes_accessed=16 * block * block * terms, transcendentals=0
    )


def routes(tick, columns, sites, sectors):
    relay, lift, far_one, far_two, stay = [], [], [], [], []
    for site in range(min(sites - 1, tick + TICKS)):
        for sector in range(sectors):
            here = site * sectors + sector
            after = (sector + 1) % sectors
            relay.append((here, site * sectors + after))
            lift.append((here, (site + 1) * sectors + after))
            stay.append((here, (site + 1) * sectors + sector))
            target = (sector + 2) % sectors
            back = (target // columns) * columns + (target + 1) % columns
            far_one.append((here, (site + 1) * sectors + back))
            far_two.append(((site + 1) * sectors + back, (site + 1) * sectors + target))
    return relay, lift, far_one, far_two, stay


def local(sites, held_env, incoming, states, weight_table, site_kind, sector_sizes, charge_shift):
    terms, block = held_env.shape[1], held_env.shape[3]
    sectors = sector_sizes.shape[0]
    columns = 4
    here = jnp.stack([lax.axis_index("site"), lax.axis_index("sector")]).astype(jnp.int32)
    place = jnp.concatenate([here, site_kind, charge_shift, sector_sizes])
    weights = weight_table.reshape(-1)
    count = states.shape[1]
    env = held_env[0, :, 0]
    parts = [shape(terms, LOW, block), shape(terms, block - LOW, block)]
    whole = shape(terms, block, block)
    split_states = [
        jax.ShapeDtypeStruct((count, 3 * block, block), jnp.bfloat16),
        jax.ShapeDtypeStruct((count, block, 3 * block), jnp.bfloat16),
    ]
    cost = estimate(block, terms)
    scalars = (place, weights)
    few = (place, weights)
    plain, turned, moved = None, None, None

    def call(kernel, inputs, outputs, aliases={}):
        specs = [SMEM if value.ndim == 1 else VMEM for value in inputs]
        specs = [HBM if value is incoming else spec for spec, value in zip(specs, inputs)]
        return pl.pallas_call(
            kernel,
            in_specs=specs,
            out_specs=[VMEM] * len(outputs),
            out_shape=outputs,
            input_output_aliases=aliases,
            compiler_params=PARAMS,
            cost_estimate=cost,
        )(*inputs)

    for tick in range(TICKS):
        relay, lift, far_one, far_two, stay = routes(tick, columns, sites, sectors)
        if tick == 0:
            two_low, two_high, plain, turned = call(
                first_kernel, scalars + (env, states), parts + split_states
            )
        else:
            two_low, two_high, env = call(
                functools.partial(gather_kernel, tick - 1),
                few + moved + (incoming, plain, turned),
                parts + [whole],
            )
        two_low = lax.ppermute(two_low, AXES, relay)
        far = lax.ppermute(two_high, AXES, far_one)
        if tick == 0:
            zero, plain, turned = call(
                first_zero_kernel,
                scalars + (env, states, plain, turned),
                [whole] + split_states,
                {4: 1, 5: 2},
            )
        else:
            (zero,) = call(zero_kernel, few + (env, plain, turned), [whole])
        kept = lax.ppermute(zero, AXES, stay)
        if tick == 0:
            one_low, one_high, plain, turned = call(
                first_one_kernel,
                scalars + (env, states, plain, turned),
                parts + split_states,
                {4: 2, 5: 3},
            )
        else:
            one_low, one_high = call(one_kernel, few + (env, plain, turned), parts)
        high = lax.ppermute(one_high, AXES, lift)
        low = lax.ppermute(one_low + two_low, AXES, lift)
        far = lax.ppermute(far, AXES, far_two)
        moved = (kept, low, high, far)
    (env,) = call(
        functools.partial(final_kernel, TICKS - 1), (place,) + moved + (incoming,), [whole]
    )
    return env[None, :, None]


def solution(mesh):
    return jax.shard_map(
        functools.partial(local, mesh.shape["site"]),
        mesh=mesh,
        in_specs=(
            P("site", None, "sector", None, None),
            P(None, None, "sector", None, None),
            P("site", None, "sector", None, None),
            P(),
            P("site"),
            P(),
            P(),
        ),
        out_specs=P("site", None, "sector", None, None),
        check_vma=False,
    )
```

```python
import functools

import jax
import jax.numpy as jnp
from jax import lax
from jax.experimental import pallas as pl
from jax.experimental.pallas import tpu as pltpu
from jax.sharding import PartitionSpec as P


TICKS = 4
AXES = ("site", "sector")
LOW = 128
VMEM = pl.BlockSpec(memory_space=pltpu.VMEM)
SMEM = pl.BlockSpec(memory_space=pltpu.SMEM)
HBM = pl.BlockSpec(memory_space=pltpu.HBM)
PARAMS = pltpu.CompilerParams(vmem_limit_bytes=24 * 1024 * 1024)


def halves(value):
    high = value.astype(jnp.bfloat16)
    return high, (value - high.astype(jnp.float32)).astype(jnp.bfloat16)


def dot(left, right):
    return jnp.dot(left, right, preferred_element_type=jnp.float32)


def shift_of(place, state):
    return place[3 + state]


def fill(state, place, count, states_ref, plain_ref, turned_ref):
    block = states_ref.shape[-1]
    owner = place[1]
    sectors = place.shape[0] - 3 - count
    live_in = place[3 + count + owner]
    live_out = place[3 + count + lax.rem(owner + shift_of(place, state), sectors)]
    rows = lax.broadcasted_iota(jnp.int32, (block, block), 0)
    columns = lax.broadcasted_iota(jnp.int32, (block, block), 1)
    keep = (rows < live_in) & (columns < live_out)
    masked = jnp.where(keep, states_ref[0, state, 0], jnp.float32(0.0))
    high, low = halves(masked)
    plain_ref[state, 0:block, :] = high
    plain_ref[state, block : 2 * block, :] = low
    plain_ref[state, 2 * block :, :] = high
    high, low = halves(masked.T)
    turned_ref[state, :, 0:block] = high
    turned_ref[state, :, block : 2 * block] = high
    turned_ref[state, :, 2 * block :] = low


def each_state(offset, place, count, body):
    def one_state(state, found):
        mine = shift_of(place, state) == offset

        @pl.when(mine)
        def _():
            body(state, found == 0)

        return found + mine.astype(jnp.int32)

    lax.fori_loop(0, count, one_state, jnp.int32(0))


def mix(place, weights, count, state, out_term, env_refs):
    pieces = []
    for ref in env_refs:
        terms = ref.shape[0]
        base = (place[2] * count + state) * terms * terms + out_term
        mixed = weights[base] * ref[0]
        for term in range(1, terms):
            mixed += weights[base + term * terms] * ref[term]
        pieces.append(mixed)
    return pieces[0] if len(pieces) == 1 else jnp.concatenate(pieces, axis=0)


def products(offset, place, weights, env_refs, plain_ref, turned_ref, stores, ready=None):
    count = plain_ref.shape[0]

    def body(state, first):
        if ready is not None:
            ready(state)

        @pl.loop(0, env_refs[0].shape[0])
        def _(out_term):
            high, low = halves(mix(place, weights, count, state, out_term, env_refs))
            right = dot(turned_ref[state], jnp.concatenate([high, low, high], axis=0))
            high, low = halves(right)
            triple = dot(jnp.concatenate([high, high, low], axis=1), plain_ref[state])
            row = 0
            for ref in stores:
                rows = ref.shape[1]
                before = jnp.where(first, jnp.float32(0.0), ref[out_term])
                ref[out_term] = before + triple[row : row + rows]
                row += rows

    each_state(offset, place, count, body)


def row_products(place, weights, env_ref, start, plain_ref, turned_ref, combine):
    count = plain_ref.shape[0]
    rows, block = env_ref.shape[1], env_ref.shape[2]

    def body(state, first):
        @pl.loop(0, env_ref.shape[0])
        def _(out_term):
            high, low = halves(mix(place, weights, count, state, out_term, [env_ref]))
            right = dot(jnp.concatenate([high, high, low], axis=1), plain_ref[state])
            high, low = halves(right)
            left = [
                turned_ref[state, :, part * block + start : part * block + start + rows]
                for part in range(3)
            ]
            triple = dot(
                jnp.concatenate(left, axis=1), jnp.concatenate([high, low, high], axis=0)
            )
            combine(out_term, triple, first)

    each_state(2, place, count, body)


def early_kernel(tick, place, weights, stay, high, far_a, far_b, incoming, plain, turned,
                 env_high, part):
    @pl.when(place[0] == 0)
    def _():
        pltpu.sync_copy(incoming.at[tick, :, 0, LOW:], env_high)

    @pl.when(place[0] != 0)
    def _():
        half = far_a.shape[1]
        env_high[:, :half] = stay[:, LOW : LOW + half] + high[:, :half] + far_a[...]
        env_high[:, half:] = stay[:, LOW + half :] + high[:, half:] + far_b[...]

    def combine(term, value, first):
        part[term] = jnp.where(first, jnp.float32(0.0), part[term]) + value

    row_products(place, weights, env_high, LOW, plain, turned, combine)


def late_kernel(tick, place, weights, stay, low, part, incoming, plain, turned,
                out_low, out_a, out_b, env_low):
    @pl.when(place[0] == 0)
    def _():
        pltpu.sync_copy(incoming.at[tick, :, 0, :LOW], env_low)

    @pl.when(place[0] != 0)
    def _():
        env_low[...] = stay[:, :LOW] + low[...]

    def combine(term, value, first):
        row = 0
        for ref in (out_low, out_a, out_b):
            rows = ref.shape[1]
            before = jnp.where(first, part[term, row : row + rows], ref[term])
            ref[term] = before + value[row : row + rows]
            row += rows

    row_products(place, weights, env_low, 0, plain, turned, combine)


def first_kernel(place, weights, env, states, out_low, out_a, out_b, plain, turned):
    def ready(state):
        fill(state, place, plain.shape[0], states, plain, turned)

    products(2, place, weights, [env], plain, turned, [out_low, out_a, out_b], ready)


def first_one_kernel(place, weights, env, states, plain_in, turned_in,
                     out_low, out_high, plain, turned):
    def ready(state):
        fill(state, place, plain.shape[0], states, plain, turned)

    products(1, place, weights, [env], plain, turned, [out_low, out_high], ready)


def first_zero_kernel(place, weights, env, states, plain_in, turned_in, out, plain, turned):
    def ready(state):
        fill(state, place, plain.shape[0], states, plain, turned)

    products(0, place, weights, [env], plain, turned, [out], ready)


def one_kernel(place, weights, env_low, env_high, plain, turned, out_low, out_high):
    products(1, place, weights, [env_low, env_high], plain, turned, [out_low, out_high])


def zero_kernel(place, weights, env_low, env_high, plain, turned, out):
    products(0, place, weights, [env_low, env_high], plain, turned, [out])


def final_kernel(tick, place, stay, high, far_a, far_b, low, incoming, env):
    @pl.when(place[0] == 0)
    def _():
        pltpu.sync_copy(incoming.at[tick, :, 0], env)

    @pl.when(place[0] != 0)
    def _():
        half = far_a.shape[1]
        env[:, :LOW] = stay[:, :LOW] + low[...]
        env[:, LOW : LOW + half] = stay[:, LOW : LOW + half] + high[:, :half] + far_a[...]
        env[:, LOW + half :] = stay[:, LOW + half :] + high[:, half:] + far_b[...]


def shape(*dims):
    return jax.ShapeDtypeStruct(dims, jnp.float32)


def estimate(block, terms):
    return pl.CostEstimate(
        flops=terms * 12 * block**3, bytes_accessed=16 * block * block * terms, transcendentals=0
    )


def routes(tick, columns, sites, sectors):
    relay, lift, far_one, far_two, stay = [], [], [], [], []
    for site in range(min(sites - 1, tick + TICKS)):
        for sector in range(sectors):
            here = site * sectors + sector
            after = (sector + 1) % sectors
            relay.append((here, site * sectors + after))
            lift.append((here, (site + 1) * sectors + after))
            stay.append((here, (site + 1) * sectors + sector))
            target = (sector + 2) % sectors
            back = (target // columns) * columns + (target + 1) % columns
            far_one.append((here, (site + 1) * sectors + back))
            far_two.append(((site + 1) * sectors + back, (site + 1) * sectors + target))
    return relay, lift, far_one, far_two, stay


def local(sites, held_env, incoming, states, weight_table, site_kind, sector_sizes, charge_shift):
    terms, block = held_env.shape[1], held_env.shape[3]
    sectors = sector_sizes.shape[0]
    columns = 4
    here = jnp.stack([lax.axis_index("site"), lax.axis_index("sector")]).astype(jnp.int32)
    place = jnp.concatenate([here, site_kind, charge_shift, sector_sizes])
    weights = weight_table.reshape(-1)
    count = states.shape[1]
    env = held_env[0, :, 0]
    half = (block - LOW) // 2
    parts = [shape(terms, LOW, block), shape(terms, block - LOW, block)]
    thirds = [shape(terms, LOW, block), shape(terms, half, block), shape(terms, half, block)]
    whole = shape(terms, block, block)
    split_states = [
        jax.ShapeDtypeStruct((count, 3 * block, block), jnp.bfloat16),
        jax.ShapeDtypeStruct((count, block, 3 * block), jnp.bfloat16),
    ]
    cost = estimate(block, terms)
    scalars = (place, weights)
    plain, turned = None, None

    def call(kernel, inputs, outputs, aliases={}):
        specs = [SMEM if value.ndim == 1 else VMEM for value in inputs]
        specs = [HBM if value is incoming else spec for spec, value in zip(specs, inputs)]
        return pl.pallas_call(
            kernel,
            in_specs=specs,
            out_specs=[VMEM] * len(outputs),
            out_shape=outputs,
            input_output_aliases=aliases,
            compiler_params=PARAMS,
            cost_estimate=cost,
        )(*inputs)

    for tick in range(TICKS):
        relay, lift, far_one, far_two, stay = routes(tick, columns, sites, sectors)
        if tick == 0:
            two_low, far_a, far_b, plain, turned = call(
                first_kernel, scalars + (env, states), thirds + split_states
            )
        else:
            two_low, far_a, far_b, env_low = call(
                functools.partial(late_kernel, tick - 1),
                scalars + (kept, low, part, incoming, plain, turned),
                thirds + [parts[0]],
            )
        far_a = lax.ppermute(far_a, AXES, far_one)
        two_low = lax.ppermute(two_low, AXES, relay)
        far_b = lax.ppermute(far_b, AXES, far_one)
        if tick == 0:
            one_low, one_high, plain, turned = call(
                first_one_kernel,
                scalars + (env, states, plain, turned),
                parts + split_states,
                {4: 2, 5: 3},
            )
        else:
            one_low, one_high = call(
                one_kernel, scalars + (env_low, env_high, plain, turned), parts
            )
        high = lax.ppermute(one_high, AXES, lift)
        if tick == 0:
            zero, plain, turned = call(
                first_zero_kernel,
                scalars + (env, states, plain, turned),
                [whole] + split_states,
                {4: 1, 5: 2},
            )
        else:
            (zero,) = call(zero_kernel, scalars + (env_low, env_high, plain, turned), [whole])
        kept = lax.ppermute(zero, AXES, stay)
        low = lax.ppermute(one_low + two_low, AXES, lift)
        far_a = lax.ppermute(far_a, AXES, far_two)
        far_b = lax.ppermute(far_b, AXES, far_two)
        if tick < TICKS - 1:
            env_high, part = call(
                functools.partial(early_kernel, tick),
                scalars + (kept, high, far_a, far_b, incoming, plain, turned),
                [parts[1], whole],
            )
    (env,) = call(
        functools.partial(final_kernel, TICKS - 1),
        (place, kept, high, far_a, far_b, low, incoming),
        [whole],
    )
    return env[None, :, None]


def solution(mesh):
    return jax.shard_map(
        functools.partial(local, mesh.shape["site"]),
        mesh=mesh,
        in_specs=(
            P("site", None, "sector", None, None),
            P(None, None, "sector", None, None),
            P("site", None, "sector", None, None),
            P(),
            P("site"),
            P(),
            P(),
        ),
        out_specs=P("site", None, "sector", None, None),
        check_vma=False,
    )
```

```python
import functools

import jax
import jax.numpy as jnp
from jax import lax
from jax.experimental import pallas as pl
from jax.experimental.pallas import tpu as pltpu
from jax.sharding import PartitionSpec as P


TICKS = 4
AXES = ("site", "sector")
LOW = 128
VMEM = pl.BlockSpec(memory_space=pltpu.VMEM)
SMEM = pl.BlockSpec(memory_space=pltpu.SMEM)
HBM = pl.BlockSpec(memory_space=pltpu.HBM)
PARAMS = pltpu.CompilerParams(vmem_limit_bytes=24 * 1024 * 1024)


def halves(value):
    high = value.astype(jnp.bfloat16)
    return high, (value - high.astype(jnp.float32)).astype(jnp.bfloat16)


def dot(left, right):
    return jnp.dot(left, right, preferred_element_type=jnp.float32)


def shift_of(place, state):
    return place[3 + state]


def fill(state, place, count, states_ref, plain_ref, turned_ref):
    block = states_ref.shape[-1]
    owner = place[1]
    sectors = place.shape[0] - 3 - count
    live_in = place[3 + count + owner]
    live_out = place[3 + count + lax.rem(owner + shift_of(place, state), sectors)]
    rows = lax.broadcasted_iota(jnp.int32, (block, block), 0)
    columns = lax.broadcasted_iota(jnp.int32, (block, block), 1)
    keep = (rows < live_in) & (columns < live_out)
    masked = jnp.where(keep, states_ref[0, state, 0], jnp.float32(0.0))
    high, low = halves(masked)
    plain_ref[state, 0:block, :] = high
    plain_ref[state, block : 2 * block, :] = low
    plain_ref[state, 2 * block :, :] = high
    high, low = halves(masked.T)
    turned_ref[state, :, 0:block] = high
    turned_ref[state, :, block : 2 * block] = high
    turned_ref[state, :, 2 * block :] = low


def each_state(offset, place, count, body):
    def one_state(state, found):
        mine = shift_of(place, state) == offset

        @pl.when(mine)
        def _():
            body(state, found == 0)

        return found + mine.astype(jnp.int32)

    lax.fori_loop(0, count, one_state, jnp.int32(0))


def mix(place, weights, count, state, out_term, env_refs):
    pieces = []
    for ref in env_refs:
        terms = ref.shape[0]
        base = (place[2] * count + state) * terms * terms + out_term
        mixed = weights[base] * ref[0]
        for term in range(1, terms):
            mixed += weights[base + term * terms] * ref[term]
        pieces.append(mixed)
    return pieces[0] if len(pieces) == 1 else jnp.concatenate(pieces, axis=0)


def products(offset, place, weights, env_refs, plain_ref, turned_ref, stores, scratch, ready=None):
    count = plain_ref.shape[0]
    terms, block = env_refs[0].shape[0], plain_ref.shape[2]
    wide, tall = scratch

    def body(state, first):
        if ready is not None:
            ready(state)
        for term in range(terms):
            columns = slice(term * block, (term + 1) * block)
            high, low = halves(mix(place, weights, count, state, term, env_refs))
            wide[0:block, columns] = high
            wide[block : 2 * block, columns] = low
            wide[2 * block :, columns] = high
        right = dot(turned_ref[state], wide[...])
        for term in range(terms):
            lines = slice(term * block, (term + 1) * block)
            high, low = halves(right[:, lines])
            tall[lines, 0:block] = high
            tall[lines, block : 2 * block] = high
            tall[lines, 2 * block :] = low
        triple = dot(tall[...], plain_ref[state])
        for term in range(terms):
            row = term * block
            for ref in stores:
                rows = ref.shape[1]
                before = jnp.where(first, jnp.float32(0.0), ref[term])
                ref[term] = before + triple[row : row + rows]
                row += rows

    each_state(offset, place, count, body)


def looped(offset, place, weights, env_refs, plain_ref, turned_ref, stores, ready=None):
    count = plain_ref.shape[0]

    def body(state, first):
        if ready is not None:
            ready(state)

        @pl.loop(0, env_refs[0].shape[0])
        def _(out_term):
            high, low = halves(mix(place, weights, count, state, out_term, env_refs))
            right = dot(turned_ref[state], jnp.concatenate([high, low, high], axis=0))
            high, low = halves(right)
            triple = dot(jnp.concatenate([high, high, low], axis=1), plain_ref[state])
            row = 0
            for ref in stores:
                rows = ref.shape[1]
                before = jnp.where(first, jnp.float32(0.0), ref[out_term])
                ref[out_term] = before + triple[row : row + rows]
                row += rows

    each_state(offset, place, count, body)


def row_products(place, weights, env_ref, start, plain_ref, turned_ref, combine):
    count = plain_ref.shape[0]
    rows, block = env_ref.shape[1], env_ref.shape[2]

    def body(state, first):
        @pl.loop(0, env_ref.shape[0])
        def _(out_term):
            high, low = halves(mix(place, weights, count, state, out_term, [env_ref]))
            right = dot(jnp.concatenate([high, high, low], axis=1), plain_ref[state])
            high, low = halves(right)
            left = [
                turned_ref[state, :, part * block + start : part * block + start + rows]
                for part in range(3)
            ]
            triple = dot(
                jnp.concatenate(left, axis=1), jnp.concatenate([high, low, high], axis=0)
            )
            combine(out_term, triple, first)

    each_state(2, place, count, body)


def early_kernel(tick, place, weights, stay, high, far_a, far_b, incoming, plain, turned,
                 env_high, part, *scratch):
    @pl.when(place[0] == 0)
    def _():
        pltpu.sync_copy(incoming.at[tick, :, 0, LOW:], env_high)

    @pl.when(place[0] != 0)
    def _():
        half = far_a.shape[1]
        env_high[:, :half] = stay[:, :half] + high[:, :half] + far_a[...]
        env_high[:, half:] = stay[:, half:] + high[:, half:] + far_b[...]

    def combine(term, value, first):
        part[term] = jnp.where(first, jnp.float32(0.0), part[term]) + value

    row_products(place, weights, env_high, LOW, plain, turned, combine)


def late_kernel(tick, place, weights, stay, low, part, incoming, plain, turned,
                out_low, out_a, out_b, env_low, *scratch):
    @pl.when(place[0] == 0)
    def _():
        pltpu.sync_copy(incoming.at[tick, :, 0, :LOW], env_low)

    @pl.when(place[0] != 0)
    def _():
        env_low[...] = stay[...] + low[...]

    def combine(term, value, first):
        row = 0
        for ref in (out_low, out_a, out_b):
            rows = ref.shape[1]
            before = jnp.where(first, part[term, row : row + rows], ref[term])
            ref[term] = before + value[row : row + rows]
            row += rows

    row_products(place, weights, env_low, 0, plain, turned, combine)


def first_kernel(place, weights, env, states, out_low, out_a, out_b, plain, turned,
                 *scratch):
    def ready(state):
        fill(state, place, plain.shape[0], states, plain, turned)

    products(2, place, weights, [env], plain, turned, [out_low, out_a, out_b], scratch,
             ready)


def first_one_kernel(place, weights, env, states, plain_in, turned_in,
                     out_low, out_high, plain, turned, *scratch):
    def ready(state):
        fill(state, place, plain.shape[0], states, plain, turned)

    products(1, place, weights, [env], plain, turned, [out_low, out_high], scratch, ready)


def first_zero_kernel(place, weights, env, states, plain_in, turned_in,
                      out_low, out_high, plain, turned, *scratch):
    def ready(state):
        fill(state, place, plain.shape[0], states, plain, turned)

    looped(0, place, weights, [env], plain, turned, [out_low, out_high], ready)


def one_kernel(place, weights, env_low, env_high, plain, turned, out_low, out_high, *scratch):
    products(1, place, weights, [env_low, env_high], plain, turned, [out_low, out_high], scratch)


def zero_kernel(place, weights, env_low, env_high, plain, turned, out_low, out_high, *scratch):
    looped(0, place, weights, [env_low, env_high], plain, turned, [out_low, out_high])


def final_kernel(tick, place, stay_low, stay_high, high, far_a, far_b, low, incoming, env,
                 *scratch):
    @pl.when(place[0] == 0)
    def _():
        pltpu.sync_copy(incoming.at[tick, :, 0], env)

    @pl.when(place[0] != 0)
    def _():
        half = far_a.shape[1]
        env[:, :LOW] = stay_low[...] + low[...]
        env[:, LOW : LOW + half] = stay_high[:, :half] + high[:, :half] + far_a[...]
        env[:, LOW + half :] = stay_high[:, half:] + high[:, half:] + far_b[...]


def shape(*dims):
    return jax.ShapeDtypeStruct(dims, jnp.float32)


def estimate(block, terms):
    return pl.CostEstimate(
        flops=terms * 12 * block**3, bytes_accessed=16 * block * block * terms, transcendentals=0
    )


def routes(tick, columns, sites, sectors):
    relay, lift, far_one, far_two, stay = [], [], [], [], []
    for site in range(min(sites - 1, tick + TICKS)):
        for sector in range(sectors):
            here = site * sectors + sector
            after = (sector + 1) % sectors
            relay.append((here, site * sectors + after))
            lift.append((here, (site + 1) * sectors + after))
            stay.append((here, (site + 1) * sectors + sector))
            target = (sector + 2) % sectors
            back = (target // columns) * columns + (target + 1) % columns
            far_one.append((here, (site + 1) * sectors + back))
            far_two.append(((site + 1) * sectors + back, (site + 1) * sectors + target))
    return relay, lift, far_one, far_two, stay


def local(sites, held_env, incoming, states, weight_table, site_kind, sector_sizes, charge_shift):
    terms, block = held_env.shape[1], held_env.shape[3]
    sectors = sector_sizes.shape[0]
    columns = 4
    here = jnp.stack([lax.axis_index("site"), lax.axis_index("sector")]).astype(jnp.int32)
    place = jnp.concatenate([here, site_kind, charge_shift, sector_sizes])
    weights = weight_table.reshape(-1)
    count = states.shape[1]
    env = held_env[0, :, 0]
    half = (block - LOW) // 2
    parts = [shape(terms, LOW, block), shape(terms, block - LOW, block)]
    thirds = [shape(terms, LOW, block), shape(terms, half, block), shape(terms, half, block)]
    whole = shape(terms, block, block)
    split_states = [
        jax.ShapeDtypeStruct((count, 3 * block, block), jnp.bfloat16),
        jax.ShapeDtypeStruct((count, block, 3 * block), jnp.bfloat16),
    ]
    cost = estimate(block, terms)
    scalars = (place, weights)
    plain, turned = None, None

    def call(kernel, inputs, outputs, aliases={}, rows=None):
        rows = rows or block
        scratch = [(3 * rows, terms * block), (terms * rows, 3 * block)]
        specs = [SMEM if value.ndim == 1 else VMEM for value in inputs]
        specs = [HBM if value is incoming else spec for spec, value in zip(specs, inputs)]
        return pl.pallas_call(
            kernel,
            in_specs=specs,
            out_specs=[VMEM] * len(outputs),
            out_shape=outputs,
            scratch_shapes=[pltpu.VMEM(dims, jnp.bfloat16) for dims in scratch],
            input_output_aliases=aliases,
            compiler_params=PARAMS,
            cost_estimate=cost,
        )(*inputs)

    for tick in range(TICKS):
        relay, lift, far_one, far_two, stay = routes(tick, columns, sites, sectors)
        if tick == 0:
            two_low, far_a, far_b, plain, turned = call(
                first_kernel, scalars + (env, states), thirds + split_states
            )
        else:
            two_low, far_a, far_b, env_low = call(
                functools.partial(late_kernel, tick - 1),
                scalars + (kept_low, low, part, incoming, plain, turned),
                thirds + [parts[0]],
                rows=LOW,
            )
        far_a = lax.ppermute(far_a, AXES, far_one)
        two_low = lax.ppermute(two_low, AXES, relay)
        far_b = lax.ppermute(far_b, AXES, far_one)
        if tick == 0:
            one_low, one_high, plain, turned = call(
                first_one_kernel,
                scalars + (env, states, plain, turned),
                parts + split_states,
                {4: 2, 5: 3},
            )
        else:
            one_low, one_high = call(
                one_kernel, scalars + (env_low, env_high, plain, turned), parts
            )
        high = lax.ppermute(one_high, AXES, lift)
        if tick == 0:
            zero_low, zero_high, plain, turned = call(
                first_zero_kernel,
                scalars + (env, states, plain, turned),
                parts + split_states,
                {4: 2, 5: 3},
            )
        else:
            zero_low, zero_high = call(
                zero_kernel, scalars + (env_low, env_high, plain, turned), parts
            )
        kept_high = lax.ppermute(zero_high, AXES, stay)
        kept_low = lax.ppermute(zero_low, AXES, stay)
        low = lax.ppermute(one_low + two_low, AXES, lift)
        far_a = lax.ppermute(far_a, AXES, far_two)
        far_b = lax.ppermute(far_b, AXES, far_two)
        if tick < TICKS - 1:
            env_high, part = call(
                functools.partial(early_kernel, tick),
                scalars + (kept_high, high, far_a, far_b, incoming, plain, turned),
                [parts[1], whole],
                rows=block - LOW,
            )
    (env,) = call(
        functools.partial(final_kernel, TICKS - 1),
        (place, kept_low, kept_high, high, far_a, far_b, low, incoming),
        [whole],
    )
    return env[None, :, None]


def solution(mesh):
    return jax.shard_map(
        functools.partial(local, mesh.shape["site"]),
        mesh=mesh,
        in_specs=(
            P("site", None, "sector", None, None),
            P(None, None, "sector", None, None),
            P("site", None, "sector", None, None),
            P(),
            P("site"),
            P(),
            P(),
        ),
        out_specs=P("site", None, "sector", None, None),
        check_vma=False,
    )
```

```python
import functools

import jax
import jax.numpy as jnp
from jax import lax
from jax.experimental import pallas as pl
from jax.experimental.pallas import tpu as pltpu
from jax.sharding import PartitionSpec as P


TICKS = 4
AXES = ("site", "sector")
LOW = 128
VMEM = pl.BlockSpec(memory_space=pltpu.VMEM)
SMEM = pl.BlockSpec(memory_space=pltpu.SMEM)
HBM = pl.BlockSpec(memory_space=pltpu.HBM)
PARAMS = pltpu.CompilerParams(vmem_limit_bytes=24 * 1024 * 1024)


def halves(value):
    high = value.astype(jnp.bfloat16)
    return high, (value - high.astype(jnp.float32)).astype(jnp.bfloat16)


def dot(left, right):
    return jnp.dot(left, right, preferred_element_type=jnp.float32)


def shift_of(place, state):
    return place[3 + state]


def fill(state, place, count, states_ref, plain_ref, turned_ref):
    block = states_ref.shape[-1]
    owner = place[1]
    sectors = place.shape[0] - 3 - count
    live_in = place[3 + count + owner]
    live_out = place[3 + count + lax.rem(owner + shift_of(place, state), sectors)]
    rows = lax.broadcasted_iota(jnp.int32, (block, block), 0)
    columns = lax.broadcasted_iota(jnp.int32, (block, block), 1)
    keep = (rows < live_in) & (columns < live_out)
    masked = jnp.where(keep, states_ref[0, state, 0], jnp.float32(0.0))
    high, low = halves(masked)
    plain_ref[state, 0:block, :] = high
    plain_ref[state, block : 2 * block, :] = low
    plain_ref[state, 2 * block :, :] = high
    high, low = halves(masked.T)
    turned_ref[state, :, 0:block] = high
    turned_ref[state, :, block : 2 * block] = high
    turned_ref[state, :, 2 * block :] = low


def each_state(offset, place, count, body):
    def one_state(state, found):
        mine = shift_of(place, state) == offset

        @pl.when(mine)
        def _():
            body(state, found == 0)

        return found + mine.astype(jnp.int32)

    lax.fori_loop(0, count, one_state, jnp.int32(0))


def mix(place, weights, count, state, out_term, env_refs):
    pieces = []
    for ref in env_refs:
        terms = ref.shape[0]
        base = (place[2] * count + state) * terms * terms + out_term
        mixed = weights[base] * ref[0]
        for term in range(1, terms):
            mixed += weights[base + term * terms] * ref[term]
        pieces.append(mixed)
    return pieces[0] if len(pieces) == 1 else jnp.concatenate(pieces, axis=0)


def products(offset, place, weights, env_refs, plain_ref, turned_ref, stores, scratch, ready=None):
    count = plain_ref.shape[0]
    terms, block = env_refs[0].shape[0], plain_ref.shape[2]
    wide, tall = scratch

    def body(state, first):
        if ready is not None:
            ready(state)
        for term in range(terms):
            columns = slice(term * block, (term + 1) * block)
            high, low = halves(mix(place, weights, count, state, term, env_refs))
            wide[0:block, columns] = high
            wide[block : 2 * block, columns] = low
            wide[2 * block :, columns] = high
        right = dot(turned_ref[state], wide[...])
        for term in range(terms):
            lines = slice(term * block, (term + 1) * block)
            high, low = halves(right[:, lines])
            tall[lines, 0:block] = high
            tall[lines, block : 2 * block] = high
            tall[lines, 2 * block :] = low
        triple = dot(tall[...], plain_ref[state])
        for term in range(terms):
            base = term * block
            for row, ref in stores:
                rows = ref.shape[1]
                before = jnp.where(first, jnp.float32(0.0), ref[term])
                ref[term] = before + triple[base + row : base + row + rows]

    each_state(offset, place, count, body)


def looped(offset, place, weights, env_refs, plain_ref, turned_ref, stores, ready=None):
    count = plain_ref.shape[0]

    def body(state, first):
        if ready is not None:
            ready(state)

        @pl.loop(0, env_refs[0].shape[0])
        def _(out_term):
            high, low = halves(mix(place, weights, count, state, out_term, env_refs))
            right = dot(turned_ref[state], jnp.concatenate([high, low, high], axis=0))
            high, low = halves(right)
            triple = dot(jnp.concatenate([high, high, low], axis=1), plain_ref[state])
            for row, ref in stores:
                rows = ref.shape[1]
                before = jnp.where(first, jnp.float32(0.0), ref[out_term])
                ref[out_term] = before + triple[row : row + rows]

    each_state(offset, place, count, body)


def row_products(place, weights, env_ref, start, plain_ref, turned_ref, combine):
    count = plain_ref.shape[0]
    rows, block = env_ref.shape[1], env_ref.shape[2]

    def body(state, first):
        @pl.loop(0, env_ref.shape[0])
        def _(out_term):
            high, low = halves(mix(place, weights, count, state, out_term, [env_ref]))
            right = dot(jnp.concatenate([high, high, low], axis=1), plain_ref[state])
            high, low = halves(right)
            left = [
                turned_ref[state, :, part * block + start : part * block + start + rows]
                for part in range(3)
            ]
            triple = dot(
                jnp.concatenate(left, axis=1), jnp.concatenate([high, low, high], axis=0)
            )
            combine(out_term, triple, first)

    each_state(2, place, count, body)


def early_kernel(tick, place, weights, rest, kept, high, far_a, far_b, incoming, plain, turned,
                 env_high, part, *scratch):
    @pl.when(place[0] == 0)
    def _():
        pltpu.sync_copy(incoming.at[tick, :, 0, LOW:], env_high)

    @pl.when(place[0] != 0)
    def _():
        half = far_a.shape[1]
        env_high[:, :half] = kept[...] + far_a[...]
        env_high[:, half:] = rest[:, LOW:] + high[...] + far_b[...]

    def combine(term, value, first):
        part[term] = jnp.where(first, jnp.float32(0.0), part[term]) + value

    row_products(place, weights, env_high, LOW, plain, turned, combine)


def late_kernel(tick, place, weights, rest, low, part, incoming, plain, turned,
                out_low, out_a, out_b, env_low, *scratch):
    @pl.when(place[0] == 0)
    def _():
        pltpu.sync_copy(incoming.at[tick, :, 0, :LOW], env_low)

    @pl.when(place[0] != 0)
    def _():
        env_low[...] = rest[:, :LOW] + low[...]

    def combine(term, value, first):
        row = 0
        for ref in (out_low, out_a, out_b):
            rows = ref.shape[1]
            before = jnp.where(first, part[term, row : row + rows], ref[term])
            ref[term] = before + value[row : row + rows]
            row += rows

    row_products(place, weights, env_low, 0, plain, turned, combine)


def in_order(*refs):
    pairs, row = [], 0
    for ref in refs:
        pairs.append((row, ref))
        row += ref.shape[1]
    return pairs


def outer_rows(middle, rest):
    rows = middle.shape[1]
    return [(rows, middle), (0, rest.at[:, :rows]), (2 * rows, rest.at[:, rows:])]


def first_kernel(place, weights, env, states, out_low, out_a, out_b, plain, turned,
                 *scratch):
    def ready(state):
        fill(state, place, plain.shape[0], states, plain, turned)

    products(2, place, weights, [env], plain, turned, in_order(out_low, out_a, out_b), scratch,
             ready)


def first_one_kernel(place, weights, env, states, plain_in, turned_in,
                     out_low, out_a, out_b, plain, turned, *scratch):
    def ready(state):
        fill(state, place, plain.shape[0], states, plain, turned)

    products(1, place, weights, [env], plain, turned, in_order(out_low, out_a, out_b), scratch, ready)


def first_zero_kernel(place, weights, env, states, plain_in, turned_in,
                      middle, rest, plain, turned, *scratch):
    def ready(state):
        fill(state, place, plain.shape[0], states, plain, turned)

    looped(0, place, weights, [env], plain, turned, outer_rows(middle, rest), ready)


def one_kernel(place, weights, env_low, env_high, plain, turned, out_low, out_a, out_b,
               *scratch):
    products(1, place, weights, [env_low, env_high], plain, turned,
             in_order(out_low, out_a, out_b), scratch)


def zero_kernel(place, weights, env_low, env_high, plain, turned, middle, rest, *scratch):
    looped(0, place, weights, [env_low, env_high], plain, turned, outer_rows(middle, rest))


def final_kernel(tick, place, rest, kept, high, far_a, far_b, low, incoming, env,
                 *scratch):
    @pl.when(place[0] == 0)
    def _():
        pltpu.sync_copy(incoming.at[tick, :, 0], env)

    @pl.when(place[0] != 0)
    def _():
        half = far_a.shape[1]
        env[:, :LOW] = rest[:, :LOW] + low[...]
        env[:, LOW : LOW + half] = kept[...] + far_a[...]
        env[:, LOW + half :] = rest[:, LOW:] + high[...] + far_b[...]


def shape(*dims):
    return jax.ShapeDtypeStruct(dims, jnp.float32)


def estimate(block, terms):
    return pl.CostEstimate(
        flops=terms * 12 * block**3, bytes_accessed=16 * block * block * terms, transcendentals=0
    )


def routes(tick, columns, sites, sectors):
    relay, lift, far_one, far_two, stay = [], [], [], [], []
    for site in range(min(sites - 1, tick + TICKS)):
        for sector in range(sectors):
            here = site * sectors + sector
            after = (sector + 1) % sectors
            relay.append((here, site * sectors + after))
            lift.append((here, (site + 1) * sectors + after))
            stay.append((here, (site + 1) * sectors + sector))
            target = (sector + 2) % sectors
            back = (target // columns) * columns + (target + 1) % columns
            far_one.append((here, (site + 1) * sectors + back))
            far_two.append(((site + 1) * sectors + back, (site + 1) * sectors + target))
    return relay, lift, far_one, far_two, stay


def local(sites, held_env, incoming, states, weight_table, site_kind, sector_sizes, charge_shift):
    terms, block = held_env.shape[1], held_env.shape[3]
    sectors = sector_sizes.shape[0]
    columns = 4
    here = jnp.stack([lax.axis_index("site"), lax.axis_index("sector")]).astype(jnp.int32)
    place = jnp.concatenate([here, site_kind, charge_shift, sector_sizes])
    weights = weight_table.reshape(-1)
    count = states.shape[1]
    env = held_env[0, :, 0]
    half = (block - LOW) // 2
    parts = [shape(terms, LOW, block), shape(terms, block - LOW, block)]
    thirds = [shape(terms, LOW, block), shape(terms, half, block), shape(terms, half, block)]
    whole = shape(terms, block, block)
    split_states = [
        jax.ShapeDtypeStruct((count, 3 * block, block), jnp.bfloat16),
        jax.ShapeDtypeStruct((count, block, 3 * block), jnp.bfloat16),
    ]
    cost = estimate(block, terms)
    scalars = (place, weights)
    plain, turned = None, None

    def call(kernel, inputs, outputs, aliases={}, rows=None):
        rows = rows or block
        scratch = [(3 * rows, terms * block), (terms * rows, 3 * block)]
        specs = [SMEM if value.ndim == 1 else VMEM for value in inputs]
        specs = [HBM if value is incoming else spec for spec, value in zip(specs, inputs)]
        return pl.pallas_call(
            kernel,
            in_specs=specs,
            out_specs=[VMEM] * len(outputs),
            out_shape=outputs,
            scratch_shapes=[pltpu.VMEM(dims, jnp.bfloat16) for dims in scratch],
            input_output_aliases=aliases,
            compiler_params=PARAMS,
            cost_estimate=cost,
        )(*inputs)

    for tick in range(TICKS):
        relay, lift, far_one, far_two, stay = routes(tick, columns, sites, sectors)
        if tick == 0:
            two_low, far_a, far_b, plain, turned = call(
                first_kernel, scalars + (env, states), thirds + split_states
            )
        else:
            two_low, far_a, far_b, env_low = call(
                functools.partial(late_kernel, tick - 1),
                scalars + (rest, low, part, incoming, plain, turned),
                thirds + [parts[0]],
                rows=LOW,
            )
        far_a = lax.ppermute(far_a, AXES, far_one)
        two_low = lax.ppermute(two_low, AXES, relay)
        far_b = lax.ppermute(far_b, AXES, far_one)
        if tick == 0:
            one_low, one_mid, one_high, plain, turned = call(
                first_one_kernel,
                scalars + (env, states, plain, turned),
                thirds + split_states,
                {4: 3, 5: 4},
            )
        else:
            one_low, one_mid, one_high = call(
                one_kernel, scalars + (env_low, env_high, plain, turned), thirds
            )
        one_mid = lax.ppermute(one_mid, AXES, relay)
        high = lax.ppermute(one_high, AXES, lift)
        if tick == 0:
            zero_mid, zero_rest, plain, turned = call(
                first_zero_kernel,
                scalars + (env, states, plain, turned),
                parts + split_states,
                {4: 2, 5: 3},
            )
        else:
            zero_mid, zero_rest = call(
                zero_kernel, scalars + (env_low, env_high, plain, turned), parts
            )
        rest = lax.ppermute(zero_rest, AXES, stay)
        kept = lax.ppermute(zero_mid + one_mid, AXES, stay)
        low = lax.ppermute(one_low + two_low, AXES, lift)
        far_a = lax.ppermute(far_a, AXES, far_two)
        far_b = lax.ppermute(far_b, AXES, far_two)
        if tick < TICKS - 1:
            env_high, part = call(
                functools.partial(early_kernel, tick),
                scalars + (rest, kept, high, far_a, far_b, incoming, plain, turned),
                [parts[1], whole],
                rows=block - LOW,
            )
    (env,) = call(
        functools.partial(final_kernel, TICKS - 1),
        (place, rest, kept, high, far_a, far_b, low, incoming),
        [whole],
    )
    return env[None, :, None]


def solution(mesh):
    return jax.shard_map(
        functools.partial(local, mesh.shape["site"]),
        mesh=mesh,
        in_specs=(
            P("site", None, "sector", None, None),
            P(None, None, "sector", None, None),
            P("site", None, "sector", None, None),
            P(),
            P("site"),
            P(),
            P(),
        ),
        out_specs=P("site", None, "sector", None, None),
        check_vma=False,
    )
```

```python
import functools

import jax
import jax.numpy as jnp
from jax import lax
from jax.experimental import pallas as pl
from jax.experimental.pallas import tpu as pltpu
from jax.sharding import PartitionSpec as P


TICKS = 4
AXES = ("site", "sector")
LOW = 128
VMEM = pl.BlockSpec(memory_space=pltpu.VMEM)
SMEM = pl.BlockSpec(memory_space=pltpu.SMEM)
HBM = pl.BlockSpec(memory_space=pltpu.HBM)
PARAMS = pltpu.CompilerParams(vmem_limit_bytes=24 * 1024 * 1024)


def halves(value):
    high = value.astype(jnp.bfloat16)
    return high, (value - high.astype(jnp.float32)).astype(jnp.bfloat16)


def dot(left, right):
    return jnp.dot(left, right, preferred_element_type=jnp.float32)


def shift_of(place, state):
    return place[3 + state]


def fill(state, place, count, states_ref, plain_ref, turned_ref):
    block = states_ref.shape[-1]
    owner = place[1]
    sectors = place.shape[0] - 3 - count
    live_in = place[3 + count + owner]
    live_out = place[3 + count + lax.rem(owner + shift_of(place, state), sectors)]
    rows = lax.broadcasted_iota(jnp.int32, (block, block), 0)
    columns = lax.broadcasted_iota(jnp.int32, (block, block), 1)
    keep = (rows < live_in) & (columns < live_out)
    masked = jnp.where(keep, states_ref[0, state, 0], jnp.float32(0.0))
    high, low = halves(masked)
    plain_ref[state, 0:block, :] = high
    plain_ref[state, block : 2 * block, :] = low
    plain_ref[state, 2 * block :, :] = high
    high, low = halves(masked.T)
    turned_ref[state, :, 0:block] = high
    turned_ref[state, :, block : 2 * block] = high
    turned_ref[state, :, 2 * block :] = low


def each_state(offset, place, count, body):
    def one_state(state, found):
        mine = shift_of(place, state) == offset

        @pl.when(mine)
        def _():
            body(state, found == 0)

        return found + mine.astype(jnp.int32)

    lax.fori_loop(0, count, one_state, jnp.int32(0))


def mix(place, weights, count, state, out_term, env_refs):
    pieces = []
    for ref in env_refs:
        terms = ref.shape[0]
        base = (place[2] * count + state) * terms * terms + out_term
        mixed = weights[base] * ref[0]
        for term in range(1, terms):
            mixed += weights[base + term * terms] * ref[term]
        pieces.append(mixed)
    return pieces[0] if len(pieces) == 1 else jnp.concatenate(pieces, axis=0)


def products(offset, place, weights, env_refs, plain_ref, turned_ref, stores, scratch, ready=None):
    count = plain_ref.shape[0]
    terms, block = env_refs[0].shape[0], plain_ref.shape[2]
    wide, tall = scratch

    def body(state, first):
        if ready is not None:
            ready(state)
        for term in range(terms):
            columns = slice(term * block, (term + 1) * block)
            high, low = halves(mix(place, weights, count, state, term, env_refs))
            wide[0:block, columns] = high
            wide[block : 2 * block, columns] = low
            wide[2 * block :, columns] = high
        right = dot(turned_ref[state], wide[...])
        for term in range(terms):
            lines = slice(term * block, (term + 1) * block)
            high, low = halves(right[:, lines])
            tall[lines, 0:block] = high
            tall[lines, block : 2 * block] = high
            tall[lines, 2 * block :] = low
        triple = dot(tall[...], plain_ref[state])
        for term in range(terms):
            row = term * block
            for ref in stores:
                rows = ref.shape[1]
                before = jnp.where(first, jnp.float32(0.0), ref[term])
                ref[term] = before + triple[row : row + rows]
                row += rows

    each_state(offset, place, count, body)


def looped(offset, place, weights, env_refs, plain_ref, turned_ref, stores, ready=None):
    count = plain_ref.shape[0]

    def body(state, first):
        if ready is not None:
            ready(state)

        @pl.loop(0, env_refs[0].shape[0])
        def _(out_term):
            high, low = halves(mix(place, weights, count, state, out_term, env_refs))
            right = dot(turned_ref[state], jnp.concatenate([high, low, high], axis=0))
            high, low = halves(right)
            triple = dot(jnp.concatenate([high, high, low], axis=1), plain_ref[state])
            row = 0
            for ref in stores:
                rows = ref.shape[1]
                before = jnp.where(first, jnp.float32(0.0), ref[out_term])
                ref[out_term] = before + triple[row : row + rows]
                row += rows

    each_state(offset, place, count, body)


def row_products(offset, place, weights, env_ref, start, plain_ref, turned_ref, combine):
    count = plain_ref.shape[0]
    rows, block = env_ref.shape[1], env_ref.shape[2]

    def body(state, first):
        @pl.loop(0, env_ref.shape[0])
        def _(out_term):
            high, low = halves(mix(place, weights, count, state, out_term, [env_ref]))
            right = dot(jnp.concatenate([high, high, low], axis=1), plain_ref[state])
            high, low = halves(right)
            left = [
                turned_ref[state, :, part * block + start : part * block + start + rows]
                for part in range(3)
            ]
            triple = dot(
                jnp.concatenate(left, axis=1), jnp.concatenate([high, low, high], axis=0)
            )
            combine(out_term, triple, first)

    each_state(offset, place, count, body)


def early_kernel(tick, place, weights, stay, high, far_a, far_b, incoming, plain, turned,
                 env_high, part, *scratch):
    @pl.when(place[0] == 0)
    def _():
        pltpu.sync_copy(incoming.at[tick, :, 0, LOW:], env_high)

    @pl.when(place[0] != 0)
    def _():
        half = far_a.shape[1]
        env_high[:, :half] = stay[:, :half] + high[:, :half] + far_a[...]
        env_high[:, half:] = stay[:, half:] + high[:, half:] + far_b[...]

    def combine(term, value, first):
        part[term] = jnp.where(first, jnp.float32(0.0), part[term]) + value

    row_products(2, place, weights, env_high, LOW, plain, turned, combine)


def late_kernel(tick, place, weights, stay, low, part, incoming, plain, turned,
                out_low, out_a, out_b, env_low, *scratch):
    @pl.when(place[0] == 0)
    def _():
        pltpu.sync_copy(incoming.at[tick, :, 0, :LOW], env_low)

    @pl.when(place[0] != 0)
    def _():
        env_low[...] = stay[...] + low[...]

    def combine(term, value, first):
        row = 0
        for ref in (out_low, out_a, out_b):
            rows = ref.shape[1]
            before = jnp.where(first, part[term, row : row + rows], ref[term])
            ref[term] = before + value[row : row + rows]
            row += rows

    row_products(2, place, weights, env_low, 0, plain, turned, combine)


def first_kernel(place, weights, env, states, out_low, out_a, out_b, plain, turned,
                 *scratch):
    def ready(state):
        fill(state, place, plain.shape[0], states, plain, turned)

    products(2, place, weights, [env], plain, turned, [out_low, out_a, out_b], scratch,
             ready)


def first_one_kernel(place, weights, env, states, plain_in, turned_in,
                     out_low, out_high, plain, turned, *scratch):
    def ready(state):
        fill(state, place, plain.shape[0], states, plain, turned)

    looped(1, place, weights, [env], plain, turned, [out_low, out_high], ready)


def first_zero_kernel(place, weights, env, states, plain_in, turned_in,
                      out_low, out_high, plain, turned, *scratch):
    def ready(state):
        fill(state, place, plain.shape[0], states, plain, turned)

    looped(0, place, weights, [env], plain, turned, [out_low, out_high], ready)


def one_kernel(place, weights, env_low, env_high, plain, turned, out_low, out_high, *scratch):
    products(1, place, weights, [env_low, env_high], plain, turned, [out_low, out_high], scratch)


def early_zero_kernel(place, weights, env_high, plain, turned, part, *scratch):
    def combine(term, value, first):
        part[term] = jnp.where(first, jnp.float32(0.0), part[term]) + value

    row_products(0, place, weights, env_high, LOW, plain, turned, combine)


def late_zero_kernel(place, weights, env_low, part, plain, turned, out_low, out_high, *scratch):
    def combine(term, value, first):
        low = jnp.where(first, part[term, :LOW], out_low[term])
        high = jnp.where(first, part[term, LOW:], out_high[term])
        out_low[term] = low + value[:LOW]
        out_high[term] = high + value[LOW:]

    row_products(0, place, weights, env_low, 0, plain, turned, combine)


def final_kernel(tick, place, stay_low, stay_high, high, far_a, far_b, low, incoming, env,
                 *scratch):
    @pl.when(place[0] == 0)
    def _():
        pltpu.sync_copy(incoming.at[tick, :, 0], env)

    @pl.when(place[0] != 0)
    def _():
        half = far_a.shape[1]
        env[:, :LOW] = stay_low[...] + low[...]
        env[:, LOW : LOW + half] = stay_high[:, :half] + high[:, :half] + far_a[...]
        env[:, LOW + half :] = stay_high[:, half:] + high[:, half:] + far_b[...]


def shape(*dims):
    return jax.ShapeDtypeStruct(dims, jnp.float32)


def estimate(block, terms):
    return pl.CostEstimate(
        flops=terms * 12 * block**3, bytes_accessed=16 * block * block * terms, transcendentals=0
    )


def routes(tick, columns, sites, sectors):
    relay, lift, far_one, far_two, stay = [], [], [], [], []
    for site in range(min(sites - 1, tick + TICKS)):
        for sector in range(sectors):
            here = site * sectors + sector
            after = (sector + 1) % sectors
            relay.append((here, site * sectors + after))
            lift.append((here, (site + 1) * sectors + after))
            stay.append((here, (site + 1) * sectors + sector))
            target = (sector + 2) % sectors
            back = (target // columns) * columns + (target + 1) % columns
            far_one.append((here, (site + 1) * sectors + back))
            far_two.append(((site + 1) * sectors + back, (site + 1) * sectors + target))
    return relay, lift, far_one, far_two, stay


def local(sites, held_env, incoming, states, weight_table, site_kind, sector_sizes, charge_shift):
    terms, block = held_env.shape[1], held_env.shape[3]
    sectors = sector_sizes.shape[0]
    columns = 4
    here = jnp.stack([lax.axis_index("site"), lax.axis_index("sector")]).astype(jnp.int32)
    place = jnp.concatenate([here, site_kind, charge_shift, sector_sizes])
    weights = weight_table.reshape(-1)
    count = states.shape[1]
    env = held_env[0, :, 0]
    half = (block - LOW) // 2
    parts = [shape(terms, LOW, block), shape(terms, block - LOW, block)]
    thirds = [shape(terms, LOW, block), shape(terms, half, block), shape(terms, half, block)]
    whole = shape(terms, block, block)
    split_states = [
        jax.ShapeDtypeStruct((count, 3 * block, block), jnp.bfloat16),
        jax.ShapeDtypeStruct((count, block, 3 * block), jnp.bfloat16),
    ]
    cost = estimate(block, terms)
    scalars = (place, weights)
    plain, turned = None, None

    def call(kernel, inputs, outputs, aliases={}, rows=None):
        rows = rows or block
        scratch = [(3 * rows, terms * block), (terms * rows, 3 * block)]
        specs = [SMEM if value.ndim == 1 else VMEM for value in inputs]
        specs = [HBM if value is incoming else spec for spec, value in zip(specs, inputs)]
        return pl.pallas_call(
            kernel,
            in_specs=specs,
            out_specs=[VMEM] * len(outputs),
            out_shape=outputs,
            scratch_shapes=[pltpu.VMEM(dims, jnp.bfloat16) for dims in scratch],
            input_output_aliases=aliases,
            compiler_params=PARAMS,
            cost_estimate=cost,
        )(*inputs)

    for tick in range(TICKS):
        relay, lift, far_one, far_two, stay = routes(tick, columns, sites, sectors)
        if tick == 0:
            two_low, far_a, far_b, plain, turned = call(
                first_kernel, scalars + (env, states), thirds + split_states
            )
        else:
            two_low, far_a, far_b, env_low = call(
                functools.partial(late_kernel, tick - 1),
                scalars + (kept_low, low, part, incoming, plain, turned),
                thirds + [parts[0]],
                rows=LOW,
            )
        far_a = lax.ppermute(far_a, AXES, far_one)
        two_low = lax.ppermute(two_low, AXES, relay)
        far_b = lax.ppermute(far_b, AXES, far_one)
        if tick == 0:
            one_low, one_high, plain, turned = call(
                first_one_kernel,
                scalars + (env, states, plain, turned),
                parts + split_states,
                {4: 2, 5: 3},
            )
        else:
            one_low, one_high = call(
                one_kernel, scalars + (env_low, env_high, plain, turned), parts
            )
        high = lax.ppermute(one_high, AXES, lift)
        if tick == 0:
            zero_low, zero_high, plain, turned = call(
                first_zero_kernel,
                scalars + (env, states, plain, turned),
                parts + split_states,
                {4: 2, 5: 3},
            )
        else:
            zero_low, zero_high = call(
                late_zero_kernel, scalars + (env_low, zero_part, plain, turned), parts, rows=LOW
            )
        kept_high = lax.ppermute(zero_high, AXES, stay)
        kept_low = lax.ppermute(zero_low, AXES, stay)
        low = lax.ppermute(one_low + two_low, AXES, lift)
        far_a = lax.ppermute(far_a, AXES, far_two)
        far_b = lax.ppermute(far_b, AXES, far_two)
        if tick < TICKS - 1:
            env_high, part = call(
                functools.partial(early_kernel, tick),
                scalars + (kept_high, high, far_a, far_b, incoming, plain, turned),
                [parts[1], whole],
                rows=block - LOW,
            )
            (zero_part,) = call(
                early_zero_kernel, scalars + (env_high, plain, turned), [whole], rows=LOW
            )
    (env,) = call(
        functools.partial(final_kernel, TICKS - 1),
        (place, kept_low, kept_high, high, far_a, far_b, low, incoming),
        [whole],
    )
    return env[None, :, None]


def solution(mesh):
    return jax.shard_map(
        functools.partial(local, mesh.shape["site"]),
        mesh=mesh,
        in_specs=(
            P("site", None, "sector", None, None),
            P(None, None, "sector", None, None),
            P("site", None, "sector", None, None),
            P(),
            P("site"),
            P(),
            P(),
        ),
        out_specs=P("site", None, "sector", None, None),
        check_vma=False,
    )
```
